128 devices in a mesh: rowk: 8 (over y_hi, z), colk: 16 (over y_lo, x, core).
Axes of the slice: x: 4, y: 4 (y_hi: 2, y_lo: 2; y = y_hi * 2 + y_lo), z: 4, core: 2. Of those that a mesh axis runs over, the one named last changes fastest.
Arguments:
- coarse_kernel: bfloat16 [128, 128, 128, 128], P(('rowk', 'colk')), may hold values from -0.0234375 to 0.0234375
- left_rotation: bfloat16 [256, 2, 128, 128], P('rowk'), may hold values from -0.5 to 0.5
- right_rotation: bfloat16 [256, 2, 128, 128], P('colk'), may hold values from -0.5 to 0.5
- fine_map: int32 [256], replicated, may hold values from 0 to 127, as said below
- coefficient_index: int32 [256, 256, 4], P('rowk', 'colk'), may hold values from 0 to 15, as said below
- coefficient_table: float32 [16], replicated, may hold values from 0.3 to 1
- trial_vectors: bfloat16 [64, 32768], P(None, 'colk'), may hold values from -6 to 6
Outputs:
- forward_image: bfloat16 [64, 32768], P(None, ('rowk', 'colk'))
- adjoint_image: bfloat16 [64, 32768], P('rowk', 'colk')
The draws below stay inside these ranges and needn't reach their ends.
Inputs may be any that keep to these rules, and one draw needn't show every extreme that they name: `fine_map`: entry i is i // 2 or i // 2 - 1 and lies in the same aligned group of 8 coarse points as i // 2; it equals i // 2 where i // 2 is the first or the last of its group. `coefficient_index`: 0 marks an absent source; slot 0 is never 0.
All inputs are finite; a program needn't handle non-finite values.
Results may differ from the reference program's by a relative error of at most 0.018.
Values may be sent and summed in bfloat16 or wider, within the bound.
No kernel may reach another device: no remote copies, remote signals or barrier semaphores. Data moves between devices by JAX's collectives and lax.ppermute only.
A program may use at most 128 MiB of HBM per device.

```python
import jax
import jax.numpy as jnp
from jax import lax

NB = 128
VECS = 64
NCOEF = 16
NKF = 256
NKC = 128
CCOL = 8
NDIM = 32768


def draw_fine_map(key, part):
    halves = jnp.arange(NKF, dtype=jnp.int32) // 2
    steps = jax.random.randint(jax.random.fold_in(key, 11), (NKF,), 0, 2, dtype=jnp.int32)
    position = halves % CCOL
    steps = jnp.where((position == 0) | (position == CCOL - 1), 0, steps)
    return (halves - steps).astype(jnp.int32)


def draw_coefficient_index(key, part):
    base = jax.random.fold_in(key, 23)
    level_rows = jax.random.randint(jax.random.fold_in(base, 1), (NKF,), 0, 4, dtype=jnp.int32)
    level_cols = jax.random.randint(jax.random.fold_in(base, 2), (NKF,), 0, 4, dtype=jnp.int32)
    trials = jax.random.randint(jax.random.fold_in(base, 3), (NKF, NKF, 4), 0, 4, dtype=jnp.int32)
    level = jnp.maximum(level_rows[:, None], level_cols[None, :])
    keeps = trials <= level[:, :, None]
    slots = jnp.arange(4, dtype=jnp.int32)[None, None, :]
    keeps = keeps | (slots == 0)
    values = jax.random.randint(jax.random.fold_in(base, 4), (NKF, NKF, 4), 1, NCOEF, dtype=jnp.int32)
    return jnp.where(keeps, values, 0).astype(jnp.int32)


def block_scale(rng, dims, cuts, smallest, high):
    gain, own = 1.0, jax.random.fold_in(rng, 6)
    for axis_at, shards_of in cuts:
        steps = jnp.exp(jax.random.uniform(jax.random.fold_in(own, axis_at), (shards_of,), jnp.float32, smallest / len(cuts), high / len(cuts)))
        gain = gain * jnp.repeat(steps, dims[axis_at] // shards_of).reshape([-1 if axis == axis_at else 1 for axis in range(len(dims))])
    return gain


def gaussian(key, dims, scale, bound, shards=(), held_as=jnp.bfloat16):
    array = jax.random.normal(key, dims, jnp.float32) * scale
    if len(shards) > 0:
        array = block_scale(key, dims, shards, -0.22, 0.18) * array
    return jnp.clip(array, min=-bound, max=bound).astype(held_as)


def setup_inputs(seed: int = 0) -> dict:
    key_of = jax.random.split(jax.random.key(seed), 8)
    return {
        "coarse_kernel": gaussian(key_of[0], (NKC, NKC, NB, NB), (2 * NKF * NB) ** -0.5, 0.0234375, ((0, 128),)),
        "left_rotation": gaussian(key_of[1], (NKF, 2, NB, NB), NB ** -0.5, 0.5, ((0, 8),)),
        "right_rotation": gaussian(key_of[2], (NKF, 2, NB, NB), NB ** -0.5, 0.5, ((0, 16),)),
        "fine_map": draw_fine_map(jax.random.fold_in(key_of[7], 71), 0),
        "coefficient_index": draw_coefficient_index(jax.random.fold_in(key_of[7], 71), 0),
        "coefficient_table": jnp.clip(jax.random.uniform(key_of[5], (NCOEF,), jnp.float32, 0.3, 1.0), 0.3, 1.0),
        "trial_vectors": gaussian(key_of[6], (VECS, NDIM), 1.0, 6.0, ((1, 16),)),
    }


def reference(coarse_kernel, left_rotation, right_rotation, fine_map, coefficient_index, coefficient_table, trial_vectors):
    picked = coefficient_table[coefficient_index]
    weight = jnp.where(coefficient_index > 0, picked, jnp.zeros_like(picked)).astype(jnp.float32)
    offsets = jnp.arange(2, dtype=jnp.int32)
    col_source = ((fine_map[:, None] + offsets[None, :]) % NKC).astype(jnp.int32)

    def tile_row(index):
        row_source = ((fine_map[index] + offsets) % NKC).astype(jnp.int32)
        blocks = coarse_kernel[row_source[:, None, None], col_source[None, :, :]]
        shared = jnp.einsum('pjqab,jqbc->pjqac', blocks.astype(jnp.float32), right_rotation.astype(jnp.float32)).astype(jnp.bfloat16)
        row_weight = weight[index].reshape(NKF, 2, 2).transpose(1, 0, 2)
        mixed = (row_weight[:, :, 0, None, None] * shared[:, :, 0] + row_weight[:, :, 1, None, None] * shared[:, :, 1]).astype(jnp.bfloat16)
        rotor = left_rotation[index].astype(jnp.float32)
        return jnp.einsum('pba,pjbc->jac', rotor, mixed.astype(jnp.float32)).astype(jnp.bfloat16)

    vec_cols = trial_vectors.reshape(VECS, NKF, NB).astype(jnp.float32)

    def forward_row(index):
        tiles = tile_row(index).astype(jnp.float32)
        return jnp.einsum('jac,vjc->va', tiles, vec_cols)

    forward_rows = lax.map(forward_row, jnp.arange(NKF, dtype=jnp.int32))
    forward_image = forward_rows.transpose(1, 0, 2).reshape(VECS, NKF * NB).astype(jnp.bfloat16)
    forward_three = forward_image.reshape(VECS, NKF, NB).astype(jnp.float32)

    def back_step(total, index):
        tiles = tile_row(index).astype(jnp.float32)
        rows_now = forward_three[:, index, :]
        return total + jnp.einsum('jac,va->vjc', tiles, rows_now), None

    start_total = jnp.zeros((VECS, NKF, NB), jnp.float32)
    total, unused = lax.scan(back_step, start_total, jnp.arange(NKF, dtype=jnp.int32))
    adjoint_image = total.reshape(VECS, NKF * NB).astype(jnp.bfloat16)
    return forward_image, adjoint_image
```

```python
import jax
import jax.numpy as jnp
from jax import lax
from jax.experimental import pallas as pl
from jax.experimental.pallas import tpu as pltpu
from jax.sharding import PartitionSpec as P

VMEM = pl.BlockSpec(memory_space=pltpu.VMEM)
SMEM = pl.BlockSpec(memory_space=pltpu.SMEM)
NT = (((1,), (1,)), ((), ()))


def dot(left, right):
    return jnp.dot(left, right, preferred_element_type=jnp.float32)


def dot_nt(left, right):
    return lax.dot_general(left, right, NT, preferred_element_type=jnp.float32)


def shifted(value, axis, steps):
    count = lax.axis_size(axis)
    pairs = [(source, (source + steps) % count) for source in range(count)]
    return lax.ppermute(value, axis, pairs)


def rotate_kernel(x_ref, right_ref, out_ref):
    fine_cols = right_ref.shape[0]
    nb = right_ref.shape[2]
    for j in range(fine_cols):
        x_now = x_ref[:, j * nb : (j + 1) * nb]
        for dq in range(2):
            out_ref[2 * j + dq] = dot_nt(x_now, right_ref[j, dq]).astype(jnp.bfloat16)


def forward_kernel(
    index_ref, table_ref, rows_ref, cols_ref, u_ref, blocks_ref, rim_row_ref, rim_col_ref, corner_ref, left_ref, out_ref, z_ref
):
    n_p, n_q = blocks_ref.shape[:2]
    n_pairs = u_ref.shape[0]
    fine_cols = n_pairs // 2
    nb = blocks_ref.shape[-1]
    n_dest = out_ref.shape[0]
    own = left_ref.shape[0] // n_dest

    def spread(pair, carry):
        q = cols_ref[pair // 2] + pair % 2
        u_now = u_ref[pair]
        for p in range(n_p):
            z_ref[p, pair] = dot_nt(u_now, blocks_ref[p, q])
        z_ref[n_p, pair] = dot_nt(u_now, rim_row_ref[q])
        return carry

    def spread_rim(pair):
        u_now = u_ref[pair]
        for p in range(n_p):
            z_ref[p, pair] = dot_nt(u_now, rim_col_ref[p])
        z_ref[n_p, pair] = dot_nt(u_now, corner_ref[...])

    lax.fori_loop(0, n_pairs - 3, spread, 0)
    spread(n_pairs - 2, 0)
    spread_rim(n_pairs - 3)
    spread_rim(n_pairs - 1)

    def finish(dest, carry):
        for step in range(own):
            i = dest * own + step
            total = None
            for dp in range(2):
                p = rows_ref[i] + dp
                acc = None
                for pair in range(n_pairs):
                    where = (i * fine_cols + pair // 2) * 4 + 2 * dp + pair % 2
                    term = table_ref[index_ref[where]] * z_ref[p, pair]
                    acc = term if acc is None else acc + term
                part = dot(acc.astype(jnp.bfloat16), left_ref[i, dp])
                total = part if total is None else total + part
            out_ref[dest, :, step * nb : (step + 1) * nb] = total.astype(jnp.bfloat16)
        return carry

    lax.fori_loop(0, n_dest, finish, 0)


def adjoint_kernel(
    index_ref, table_ref, rows_ref, cols_ref, y_ref, blocks_ref, rim_row_ref, rim_col_ref, corner_ref, left_ref, right_ref, out_ref, z_ref
):
    n_p, n_q = blocks_ref.shape[:2]
    fine_rows = left_ref.shape[0]
    fine_cols = right_ref.shape[0]
    nb = blocks_ref.shape[-1]
    n_dest = y_ref.shape[0]
    own = fine_rows // n_dest

    def source(i, dp, y_now):
        return dot_nt(y_now, left_ref[i, dp]).astype(jnp.bfloat16)

    def y_of(dest, step):
        return y_ref[dest, :, step * nb : (step + 1) * nb]

    def spread(dest, carry):
        for step in range(own):
            i = dest * own + step
            y_now = y_of(dest, step)
            for dp in range(2):
                s_now = source(i, dp, y_now)
                p = rows_ref[i] + dp
                for q in range(n_q):
                    z_ref[2 * i + dp, q] = dot(s_now, blocks_ref[p, q])
                z_ref[2 * i + dp, n_q] = dot(s_now, rim_col_ref[p])
        return carry

    lax.fori_loop(0, n_dest - 1, spread, 0)
    dest = n_dest - 1
    for step in range(own):
        i = dest * own + step
        y_now = y_of(dest, step)
        s_now = source(i, 0, y_now)
        for q in range(n_q):
            z_ref[2 * i, q] = dot(s_now, blocks_ref[n_p - 1, q])
        z_ref[2 * i, n_q] = dot(s_now, rim_col_ref[n_p - 1])
        s_now = source(i, 1, y_now)
        for q in range(n_q):
            z_ref[2 * i + 1, q] = dot(s_now, rim_row_ref[q])
        z_ref[2 * i + 1, n_q] = dot(s_now, corner_ref[...])

    for j in range(fine_cols):
        total = None
        for dq in range(2):
            q = cols_ref[j] + dq

            def gather(i, acc):
                for dp in range(2):
                    where = (i * fine_cols + j) * 4 + 2 * dp + dq
                    acc = acc + table_ref[index_ref[where]] * z_ref[2 * i + dp, q]
                return acc

            start = jnp.zeros(z_ref.shape[2:], jnp.float32)
            acc = lax.fori_loop(0, fine_rows, gather, start, unroll=8)
            part = dot(acc.astype(jnp.bfloat16), right_ref[j, dq])
            total = part if total is None else total + part
        out_ref[:, j * nb : (j + 1) * nb] = total.astype(jnp.bfloat16)


def exchange(value, axis):
    return lax.all_to_all(value, axis, split_axis=0, concat_axis=0, tiled=True)


def body(
    coarse_kernel,
    left_rotation,
    right_rotation,
    fine_map,
    coefficient_index,
    coefficient_table,
    trial_vectors,
):
    n_rows = lax.axis_size("rowk")
    n_cols = lax.axis_size("colk")
    row_id = lax.axis_index("rowk")
    col_id = lax.axis_index("colk")
    coarse_total = coarse_kernel.shape[1]
    fine_rows = left_rotation.shape[0]
    fine_cols = right_rotation.shape[0]
    nb = left_rotation.shape[2]
    vecs = trial_vectors.shape[0]
    coarse_rows = coarse_total // n_rows
    coarse_cols = coarse_total // n_cols
    own = fine_rows // n_cols

    blocks = lax.all_to_all(coarse_kernel, "colk", split_axis=1, concat_axis=0, tiled=True)
    rim_row = shifted(blocks[0:1], "rowk", -1)
    rim_col = shifted(jnp.concatenate([blocks[:, 0], rim_row[:, 0]], axis=0), "colk", -1)
    rim_row = rim_row[0]
    corner = rim_col[coarse_rows]

    rows = lax.dynamic_slice_in_dim(fine_map, row_id * fine_rows, fine_rows) - row_id * coarse_rows
    cols = lax.dynamic_slice_in_dim(fine_map, col_id * fine_cols, fine_cols) - col_id * coarse_cols
    index = coefficient_index.reshape(-1)
    entries = jnp.arange(coefficient_table.shape[0], dtype=jnp.int32)
    table = jnp.where(entries > 0, coefficient_table, jnp.zeros_like(coefficient_table))

    u = pl.pallas_call(
        rotate_kernel,
        out_shape=jax.ShapeDtypeStruct((2 * fine_cols, vecs, nb), jnp.bfloat16),
        in_specs=[VMEM, VMEM],
        out_specs=VMEM,
        name="rotate",
    )(trial_vectors, right_rotation)

    partial = pl.pallas_call(
        forward_kernel,
        out_shape=jax.ShapeDtypeStruct((n_cols, vecs, own * nb), jnp.bfloat16),
        in_specs=[SMEM] * 4 + [VMEM] * 6,
        out_specs=VMEM,
        scratch_shapes=[pltpu.VMEM((coarse_rows + 1, 2 * fine_cols, vecs, nb), jnp.float32)],
        name="forward",
    )(index, table, rows, cols, u, blocks, rim_row, rim_col, corner, left_rotation)

    forward_image = jnp.sum(exchange(partial, "colk").astype(jnp.float32), axis=0).astype(jnp.bfloat16)
    copies = lax.optimization_barrier(jnp.broadcast_to(forward_image, (n_cols, vecs, own * nb)))
    row_image = exchange(copies, "colk")

    terms = pl.pallas_call(
        adjoint_kernel,
        out_shape=jax.ShapeDtypeStruct((vecs, fine_cols * nb), jnp.bfloat16),
        in_specs=[SMEM] * 4 + [VMEM] * 7,
        out_specs=VMEM,
        scratch_shapes=[pltpu.VMEM((2 * fine_rows, coarse_cols + 1, vecs, nb), jnp.float32)],
        name="adjoint",
    )(index, table, rows, cols, row_image, blocks, rim_row, rim_col, corner, left_rotation, right_rotation)

    terms = terms.reshape(n_rows, vecs // n_rows, fine_cols * nb)
    adjoint_image = jnp.sum(exchange(terms, "rowk").astype(jnp.float32), axis=0).astype(jnp.bfloat16)
    return (forward_image, adjoint_image)


def solution(mesh):
    return jax.shard_map(
        body,
        mesh=mesh,
        in_specs=(
            P(("rowk", "colk"), None, None, None),
            P("rowk", None, None, None),
            P("colk", None, None, None),
            P(),
            P("rowk", "colk", None),
            P(),
            P(None, "colk"),
        ),
        out_specs=(P(None, ("rowk", "colk")), P("rowk", "colk")),
        check_vma=False,
    )
```

```python
import jax
import jax.numpy as jnp
from jax import lax
from jax.experimental import pallas as pl
from jax.experimental.pallas import tpu as pltpu
from jax.sharding import PartitionSpec as P

VMEM = pl.BlockSpec(memory_space=pltpu.VMEM)
SMEM = pl.BlockSpec(memory_space=pltpu.SMEM)
NT = (((1,), (1,)), ((), ()))
BF16 = jnp.bfloat16
F32 = jnp.float32
MIB = 1 << 20


def dot(left, right):
    return jnp.dot(left, right, preferred_element_type=F32)


def dot_nt(left, right):
    return lax.dot_general(left, right, NT, preferred_element_type=F32)


def tree(terms):
    while len(terms) > 1:
        paired = [terms[k] + terms[k + 1] for k in range(0, len(terms) - 1, 2)]
        terms = paired + terms[len(terms) - len(terms) % 2 :]
    return terms[0]


def fold(value):
    half = value.shape[0] // 2
    return jnp.concatenate([value[:half], value[half:]], axis=1)


def unfold(value):
    half = value.shape[1] // 2
    return jnp.concatenate([value[:, :half], value[:, half:]], axis=0)


def shifted(value, axis, steps):
    count = lax.axis_size(axis)
    pairs = [(source, (source + steps) % count) for source in range(count)]
    return lax.ppermute(value, axis, pairs)


def rotate_kernel(x_ref, right_ref, out_ref):
    nb = right_ref.shape[2]
    for j in range(right_ref.shape[0]):
        x_now = x_ref[:, j * nb : (j + 1) * nb]
        for dq in range(2):
            out_ref[2 * j + dq] = dot_nt(x_now, right_ref[j, dq])


def prepare_kernel(index_ref, table_ref, cols_ref, u_ref, g_ref, splat_ref):
    n_pairs = u_ref.shape[0]
    fine_cols = n_pairs // 2
    nb = u_ref.shape[2]
    n_q = fine_cols // 2
    fine_rows = g_ref.shape[0] // 2

    def mix(i, carry):
        for dp in range(2):
            row = 2 * i + dp
            weights = []
            for pair in range(n_pairs):
                weight = table_ref[index_ref[(i * fine_cols + pair // 2) * 4 + 2 * dp + pair % 2]]
                weights.append(weight)
                splat_ref[row * n_pairs + pair] = jnp.full(splat_ref.shape[1:], weight, F32).astype(BF16)
            for q in range(n_q):
                total = None
                for dq in range(2):
                    if q < dq:
                        continue
                    first = 2 * (q - dq)
                    for j in range(first, min(first + 4, fine_cols)):
                        factor = jnp.where(cols_ref[j] + dq == q, weights[2 * j + dq], 0.0)
                        term = factor * u_ref[2 * j + dq]
                        total = term if total is None else total + term
                g_ref[row, :, q * nb : (q + 1) * nb] = total.astype(BF16)
        return carry

    lax.fori_loop(0, fine_rows, mix, 0)


CHUNKS = 8


def forward_kernel(rows_ref, foreign_ref, foreign_u_ref, left_ref, g_any, blocks_any, out_ref, tail_ref, g_ref, blocks_ref, t_ref, g_sem, b_sem):
    n_p, n_q, nb = blocks_ref.shape[:3]
    fine_rows = rows_ref.shape[0]
    n_dest = out_ref.shape[0]
    own = fine_rows // n_dest
    g_part = 2 * fine_rows // CHUNKS
    b_part = n_p // CHUNKS

    def g_copy(k):
        part = pl.ds(k * g_part, g_part)
        return pltpu.make_async_copy(g_any.at[part], g_ref.at[part], g_sem.at[k])

    def b_copy(k):
        part = pl.ds(k * b_part, b_part)
        return pltpu.make_async_copy(blocks_any.at[part], blocks_ref.at[part], b_sem.at[k])

    b_copy(0).start()
    for k in range(CHUNKS):
        g_copy(k).start()
        if k + 1 < CHUNKS:
            b_copy(k + 1).start()
    b_copy(0).wait()

    def whole(row):
        extra = foreign_ref[2 * row] * foreign_u_ref[0] + foreign_ref[2 * row + 1] * foreign_u_ref[1]
        first = (g_ref[row, :, :nb].astype(F32) + extra).astype(BF16)
        return jnp.concatenate([first, g_ref[row, :, nb:]], axis=1)

    def apply_some(k, carry):
        g_copy(k).wait()

        @pl.when(k + 1 < CHUNKS)
        def _():
            b_copy(k + 1).wait()

        for step in range(g_part // 2):
            i = k * (g_part // 2) + step
            for dp in range(2):
                p = jnp.minimum(rows_ref[i] + dp, n_p - 1)
                wide = jnp.concatenate([blocks_ref[p, q] for q in range(n_q)], axis=1)
                t_ref[i, :, dp * nb : (dp + 1) * nb] = dot_nt(whole(2 * i + dp), wide).astype(BF16)
        return carry

    lax.fori_loop(0, CHUNKS, apply_some, 0)
    for k in range(own):
        i = fine_rows - own + k
        t_ref[i, :, nb:] = jnp.zeros((t_ref.shape[1], nb), BF16)
        tail_ref[k] = whole(2 * i + 1)

    def finish_some(step, carry):
        for k in range(4):
            dest = 4 * step + k
            for half in range(own):
                i = dest * own + half
                y_now = dot(t_ref[i], left_ref[i].reshape(2 * nb, nb))
                out_ref[dest, :, half * nb : (half + 1) * nb] = y_now.astype(BF16)
        return carry

    lax.fori_loop(0, n_dest // 4, finish_some, 0)


def rim_kernel(main_ref, tail_ref, rim_row_ref, left_ref, rim_col_any, corner_any, out_ref):
    n_q, nb = rim_row_ref.shape[:2]
    last = out_ref.shape[0] - 1
    wide = jnp.concatenate([rim_row_ref[q] for q in range(n_q)], axis=1)
    for dest in range(last):
        out_ref[dest] = main_ref[dest]
    for k in range(left_ref.shape[0]):
        lanes = slice(k * nb, (k + 1) * nb)
        t_now = dot_nt(tail_ref[k], wide).astype(BF16)
        total = main_ref[last, :, lanes].astype(F32) + dot(t_now, left_ref[k])
        out_ref[last, :, lanes] = total.astype(BF16)


def adjoint_kernel(
    rows_ref,
    cols_ref,
    y_ref,
    rim_row_ref,
    rim_col_ref,
    corner_ref,
    left_ref,
    right_ref,
    splat_any,
    blocks_any,
    out_ref,
    s_ref,
    z_ref,
    splat_ref,
    blocks_ref,
    sems,
):
    n_p, n_q, nb = blocks_ref.shape[:3]
    fine_rows = left_ref.shape[0]
    fine_cols = right_ref.shape[0]
    n_dest = y_ref.shape[0]
    own = fine_rows // n_dest
    blocks_copy = pltpu.make_async_copy(blocks_any, blocks_ref, sems.at[0])
    splat_copy = pltpu.make_async_copy(splat_any, splat_ref, sems.at[1])
    blocks_copy.start()
    splat_copy.start()

    def rotate(step, carry):
        for k in range(4):
            dest = 4 * step + k
            for half in range(own):
                i = dest * own + half
                y_now = y_ref[dest, :, half * nb : (half + 1) * nb]
                for dp in range(2):
                    s_ref[2 * i + dp] = dot_nt(y_now, left_ref[i, dp]).astype(BF16)
        return carry

    lax.fori_loop(0, n_dest // 4, rotate, 0)
    blocks_copy.wait()

    def spread(row, block_of, rim):
        s_now = s_ref[row]
        for q in range(0, n_q, 2):
            moved = dot(s_now, jnp.concatenate([block_of(q), block_of(q + 1)], axis=1))
            z_ref[row, q] = fold(moved[:, :nb]).astype(BF16)
            z_ref[row, q + 1] = fold(moved[:, nb:]).astype(BF16)
        z_ref[row, n_q] = fold(dot(s_now, rim)).astype(BF16)

    def spread_row(i, dp):
        p = rows_ref[i] + dp
        spread(2 * i + dp, lambda q: blocks_ref[p, q], rim_col_ref[p])

    def spread_some(step, carry):
        for k in range(2):
            for dp in range(2):
                spread_row(2 * step + k, dp)
        return carry

    lax.fori_loop(0, fine_rows // 2 - 1, spread_some, 0)
    for i in (fine_rows - 2, fine_rows - 1):
        spread_row(i, 0)
        spread(2 * i + 1, lambda q: rim_row_ref[q], corner_ref[0])
    splat_copy.wait()

    def gather(j, carry):
        def add(group, sums):
            sums = list(sums)
            for dq in range(2):
                q = cols_ref[j] + dq
                terms = []
                for k in range(8):
                    row = 8 * group + k
                    factor = splat_ref[row * 2 * fine_cols + 2 * j + dq]
                    value = z_ref[row, q]
                    terms.append(value * jnp.concatenate([factor] * (value.shape[0] // 8), axis=0))
                sums[dq] = sums[dq] + tree(terms)
            return tuple(sums)

        start = jnp.zeros(z_ref.shape[2:], BF16)
        sums = lax.fori_loop(0, fine_rows // 4, add, (start, start))
        both = jnp.concatenate([unfold(part) for part in sums], axis=1)
        lanes = pl.ds(pl.multiple_of(j * nb, nb), nb)
        out_ref[:, lanes] = dot(both, right_ref[j].reshape(2 * nb, nb)).astype(BF16)
        return carry

    lax.fori_loop(0, fine_cols, gather, 0)


def exchange(value, axis):
    return lax.all_to_all(value, axis, split_axis=0, concat_axis=0, tiled=True)


def call(kernel, name, spaces, outs, scratch, limit, flops, args):
    specs = {"s": SMEM, "v": VMEM, "h": pl.BlockSpec(memory_space=pltpu.HBM), "a": pl.BlockSpec(memory_space=pl.ANY)}
    size = sum(a.size * a.dtype.itemsize for a in args)
    return pl.pallas_call(
        kernel,
        out_shape=[jax.ShapeDtypeStruct(shape, kind) for shape, kind in outs],
        in_specs=[specs[space] for space in spaces],
        out_specs=[VMEM] * len(outs),
        scratch_shapes=scratch,
        cost_estimate=pl.CostEstimate(flops=flops, bytes_accessed=size, transcendentals=0),
        compiler_params=pltpu.CompilerParams(vmem_limit_bytes=limit * MIB),
        name=name,
    )(*args)


def body(
    coarse_kernel,
    left_rotation,
    right_rotation,
    fine_map,
    coefficient_index,
    coefficient_table,
    trial_vectors,
):
    n_rows = lax.axis_size("rowk")
    n_cols = lax.axis_size("colk")
    row_id = lax.axis_index("rowk")
    col_id = lax.axis_index("colk")
    coarse_total = coarse_kernel.shape[1]
    fine_rows = left_rotation.shape[0]
    fine_cols = right_rotation.shape[0]
    nb = left_rotation.shape[2]
    vecs = trial_vectors.shape[0]
    coarse_rows = coarse_total // n_rows
    coarse_cols = coarse_total // n_cols
    own = fine_rows // n_cols
    n_pairs = 2 * fine_cols
    dma = pltpu.SemaphoreType.DMA

    blocks = exchange(coarse_kernel.reshape(n_cols, coarse_cols, nb, nb), "colk")

    rows = lax.dynamic_slice_in_dim(fine_map, row_id * fine_rows, fine_rows) - row_id * coarse_rows
    cols = lax.dynamic_slice_in_dim(fine_map, col_id * fine_cols, fine_cols) - col_id * coarse_cols
    entries = jnp.arange(coefficient_table.shape[0], dtype=jnp.int32)
    table = jnp.where(entries > 0, coefficient_table, jnp.zeros_like(coefficient_table))
    edge = coefficient_index[:, fine_cols - 2 :, 1::2].transpose(0, 2, 1).reshape(-1)
    edge = jnp.sum(jnp.where(edge[:, None] == entries, table, jnp.zeros_like(table)), axis=-1)
    (u,) = call(rotate_kernel, "rotate", "vv", [((n_pairs, vecs, nb), F32)], [], 4, 10**8, (trial_vectors, right_rotation))
    foreign = shifted(edge, "colk", 1)
    foreign_u = shifted(jnp.stack([u[n_pairs - 3], u[n_pairs - 1]]), "colk", 1)
    g, splat = call(
        prepare_kernel,
        "prepare",
        "sssv",
        [((2 * fine_rows, vecs, coarse_cols * nb), BF16), ((2 * fine_rows * n_pairs, 8, 2 * nb), BF16)],
        [],
        24,
        10**9,
        (coefficient_index.reshape(-1), table, cols, u),
    )
    blocks, g, splat, rows, cols = lax.optimization_barrier((blocks, g, splat, rows, cols))

    rim_row = shifted(blocks[0], "rowk", -1)
    rim_col = shifted(blocks[:, 0], "colk", -1)
    pairs = []
    for r in range(n_rows):
        for c in range(n_cols):
            pairs.append((((r + 1) % n_rows) * n_cols + (c + 1) % n_cols, r * n_cols + c))
    corner = lax.ppermute(blocks[0, 0:1], ("rowk", "colk"), pairs)

    block_buffer = pltpu.VMEM((coarse_rows, coarse_cols, nb, nb), BF16)
    main, tail = call(
        forward_kernel,
        "forward",
        "ssvvhh",
        [((n_cols, vecs, own * nb), BF16), ((own, vecs, coarse_cols * nb), BF16)],
        [
            pltpu.VMEM((2 * fine_rows, vecs, coarse_cols * nb), BF16),
            block_buffer,
            pltpu.VMEM((fine_rows, vecs, 2 * nb), BF16),
            dma((CHUNKS,)),
            dma((CHUNKS,)),
        ],
        52,
        10**9,
        (rows, foreign, foreign_u, left_rotation, g, blocks),
    )
    (partial,) = call(
        rim_kernel,
        "rim",
        "vvvvaa",
        [((n_cols, vecs, own * nb), BF16)],
        [],
        8,
        10**8,
        (main, tail, rim_row, left_rotation[fine_rows - own :, 1], rim_col, corner),
    )

    forward_image = jnp.sum(exchange(partial, "colk").astype(F32), axis=0).astype(BF16)
    copies = lax.optimization_barrier(jnp.broadcast_to(forward_image, (n_cols, vecs, own * nb)))
    row_image = exchange(copies, "colk")

    (terms,) = call(
        adjoint_kernel,
        "adjoint",
        "ssvvvvvvhh",
        [((vecs, fine_cols * nb), BF16)],
        [
            pltpu.VMEM((2 * fine_rows, vecs, nb), BF16),
            pltpu.VMEM((2 * fine_rows, coarse_cols + 1, vecs // 2, 2 * nb), BF16),
            pltpu.VMEM((2 * fine_rows * n_pairs, 8, 2 * nb), BF16),
            block_buffer,
            dma((2,)),
        ],
        52,
        10**9,
        (rows, cols, row_image, rim_row, rim_col, corner, left_rotation, right_rotation, splat, blocks),
    )

    terms = terms.reshape(n_rows, vecs // n_rows, fine_cols * nb)
    adjoint_image = jnp.sum(exchange(terms, "rowk").astype(F32), axis=0).astype(BF16)
    return (forward_image, adjoint_image)


def solution(mesh):
    return jax.shard_map(
        body,
        mesh=mesh,
        in_specs=(
            P(("rowk", "colk"), None, None, None),
            P("rowk", None, None, None),
            P("colk", None, None, None),
            P(),
            P("rowk", "colk", None),
            P(),
            P(None, "colk"),
        ),
        out_specs=(P(None, ("rowk", "colk")), P("rowk", "colk")),
        check_vma=False,
    )
```

```python
import jax
import jax.numpy as jnp
from jax import lax
from jax.experimental import pallas as pl
from jax.experimental.pallas import tpu as pltpu
from jax.sharding import PartitionSpec as P

VMEM = pl.BlockSpec(memory_space=pltpu.VMEM)
SMEM = pl.BlockSpec(memory_space=pltpu.SMEM)
NT = (((1,), (1,)), ((), ()))
BF16 = jnp.bfloat16
F32 = jnp.float32
MIB = 1 << 20


def dot(left, right):
    return jnp.dot(left, right, preferred_element_type=F32)


def dot_nt(left, right):
    return lax.dot_general(left, right, NT, preferred_element_type=F32)


def tree(terms):
    while len(terms) > 1:
        paired = [terms[k] + terms[k + 1] for k in range(0, len(terms) - 1, 2)]
        terms = paired + terms[len(terms) - len(terms) % 2 :]
    return terms[0]


def fold(value):
    half = value.shape[0] // 2
    return jnp.concatenate([value[:half], value[half:]], axis=1)


def unfold(value):
    half = value.shape[1] // 2
    return jnp.concatenate([value[:, :half], value[:, half:]], axis=0)


def shifted(value, axis, steps):
    count = lax.axis_size(axis)
    pairs = [(source, (source + steps) % count) for source in range(count)]
    return lax.ppermute(value, axis, pairs)


def rotate_kernel(x_ref, right_ref, out_ref):
    nb = right_ref.shape[2]
    for j in range(right_ref.shape[0]):
        x_now = x_ref[:, j * nb : (j + 1) * nb]
        for dq in range(2):
            out_ref[2 * j + dq] = dot_nt(x_now, right_ref[j, dq])


def prepare_kernel(index_ref, table_ref, cols_ref, order_ref, u_ref, g_ref, splat_ref):
    n_pairs = u_ref.shape[0]
    fine_cols = n_pairs // 2
    nb = u_ref.shape[2]
    n_q = fine_cols // 2
    def mix(place, carry):
        row = order_ref[place]
        base = (row // 2) * fine_cols * 4 + 2 * (row % 2)
        weights = []
        for pair in range(n_pairs):
            weight = table_ref[index_ref[base + (pair // 2) * 4 + pair % 2]]
            weights.append(weight)
            splat_ref[pair * g_ref.shape[0] + row] = jnp.full(splat_ref.shape[1:], weight, F32).astype(BF16)
        for q in range(n_q):
            total = None
            for dq in range(2):
                if q < dq:
                    continue
                first = 2 * (q - dq)
                for j in range(first, min(first + 4, fine_cols)):
                    factor = jnp.where(cols_ref[j] + dq == q, weights[2 * j + dq], 0.0)
                    term = factor * u_ref[2 * j + dq]
                    total = term if total is None else total + term
            g_ref[place, :, q * nb : (q + 1) * nb] = total.astype(BF16)
        return carry

    lax.fori_loop(0, g_ref.shape[0], mix, 0)


CHUNKS = 8


def forward_kernel(
    order_ref,
    place_ref,
    start_ref,
    foreign_ref,
    foreign_u_ref,
    left_any,
    g_any,
    blocks_any,
    out_ref,
    tail_ref,
    g_ref,
    blocks_ref,
    t_ref,
    left_ref,
    g_sem,
    b_sem,
    left_sem,
):
    n_p, n_q, nb = blocks_ref.shape[:3]
    n_rows = order_ref.shape[0]
    vecs = g_ref.shape[1]
    n_dest = out_ref.shape[0]
    own = n_rows // 2 // n_dest
    g_part = n_rows // CHUNKS
    b_part = n_p // CHUNKS

    def g_copy(k):
        part = pl.ds(k * g_part, g_part)
        return pltpu.make_async_copy(g_any.at[part], g_ref.at[part], g_sem.at[k])

    def b_copy(k):
        part = pl.ds(k * b_part, b_part)
        return pltpu.make_async_copy(blocks_any.at[part], blocks_ref.at[part], b_sem.at[k])

    for k in range(CHUNKS):
        b_copy(k).start()
        g_copy(k).start()
    left_copy = pltpu.make_async_copy(left_any, left_ref, left_sem.at[0])
    left_copy.start()

    def whole(at):
        row = order_ref[jnp.minimum(at, n_rows - 1)]
        extra = foreign_ref[2 * row] * foreign_u_ref[0] + foreign_ref[2 * row + 1] * foreign_u_ref[1]
        first = (g_ref[at, :, :nb].astype(F32) + extra).astype(BF16)
        return jnp.concatenate([first, g_ref[at, :, nb:]], axis=1)

    def apply(p):
        wide = jnp.concatenate([blocks_ref[p, q] for q in range(n_q)], axis=1)
        first = start_ref[p]

        def some(at, count):
            lines = jnp.concatenate([whole(at + k) for k in range(count)], axis=0)
            moved = dot_nt(lines, wide).astype(BF16)
            for k in range(count):
                t_ref[at + k] = moved[k * vecs : (k + 1) * vecs]

        some(first, 4)

        @pl.when(start_ref[p + 1] > first + 4)
        def _():
            some(first + 4, 2)

    def step(k, carry):
        b_copy(k).wait()

        @pl.when(k == 0)
        def _():
            g_copy(k).wait()

        @pl.when(k + 1 < CHUNKS)
        def _():
            g_copy(k + 1).wait()

        apply(2 * k)
        apply(2 * k + 1)
        return carry

    lax.fori_loop(0, CHUNKS, step, 0)
    for k in range(own):
        tail_ref[k] = whole(n_rows - own + k)
        t_ref[n_rows - own + k] = jnp.zeros(t_ref.shape[1:], BF16)
    left_copy.wait()

    def finish_some(step, carry):
        for k in range(4):
            dest = 4 * step + k
            for half in range(own):
                i = dest * own + half
                both = jnp.concatenate([t_ref[place_ref[2 * i]], t_ref[place_ref[2 * i + 1]]], axis=1)
                y_now = dot(both, left_ref[i].reshape(2 * nb, nb))
                out_ref[dest, :, half * nb : (half + 1) * nb] = y_now.astype(BF16)
        return carry

    lax.fori_loop(0, n_dest // 4, finish_some, 0)


def rim_kernel(main_ref, tail_ref, rim_row_ref, left_ref, col_any, out_ref):
    n_q, nb = rim_row_ref.shape[:2]
    last = out_ref.shape[0] - 1
    wide = jnp.concatenate([rim_row_ref[q] for q in range(n_q)], axis=1)
    for dest in range(last):
        out_ref[dest] = main_ref[dest]
    for k in range(left_ref.shape[0]):
        lanes = slice(k * nb, (k + 1) * nb)
        t_now = dot_nt(tail_ref[k], wide).astype(BF16)
        total = main_ref[last, :, lanes].astype(F32) + dot(t_now, left_ref[k])
        out_ref[last, :, lanes] = total.astype(BF16)


def adjoint_kernel(
    rows_ref,
    cols_ref,
    y_ref,
    rim_row_ref,
    rim_col_ref,
    corner_ref,
    left_ref,
    right_ref,
    splat_any,
    blocks_any,
    out_ref,
    s_ref,
    z_ref,
    splat_ref,
    blocks_ref,
    col_ref,
    sems,
):
    n_p, n_q, nb = blocks_any.shape[:3]
    fine_rows = left_ref.shape[0]
    fine_cols = right_ref.shape[0]
    n_dest = y_ref.shape[0]
    own = fine_rows // n_dest
    group = 8
    stages = list(range(0, n_q + 1, 2)) + [None]
    ends = [fine_cols if q is None else max(2 * q - 2, 0) for q in stages]
    waits = []
    for number, q in enumerate(stages):
        copies = []
        if q is not None and q < n_q:
            columns = pl.ds(q, 2)
            copies.append((blocks_any.at[:, columns], blocks_ref.at[pl.ds(0, n_p), columns]))
        begin = ends[number - 1] if number > 0 else 0
        if ends[number] > begin:
            lines = pl.ds(begin * 4 * fine_rows, (ends[number] - begin) * 4 * fine_rows)
            copies.append((splat_any.at[lines], splat_ref.at[lines]))
        started = []
        for kind, (source, target) in enumerate(copies):
            started.append(pltpu.make_async_copy(source, target, sems.at[2 * number + kind]))
            started[-1].start()
        waits.append(started)

    def rotate(step, carry):
        for k in range(4):
            dest = 4 * step + k
            for half in range(own):
                i = dest * own + half
                y_now = y_ref[dest, :, half * nb : (half + 1) * nb]
                moved = dot_nt(y_now, left_ref[i].reshape(2 * nb, nb)).astype(BF16)
                s_ref[2 * i] = moved[:, :nb]
                s_ref[2 * i + 1] = moved[:, nb:]
        return carry

    lax.fori_loop(0, n_dest // 4, rotate, 0)
    for q in range(n_q):
        blocks_ref[n_p, q] = rim_row_ref[q]
    for p in range(n_p):
        col_ref[p] = rim_col_ref[p]
    col_ref[n_p] = corner_ref[0]

    def spread(row, p, q):
        if q < n_q:
            moved = dot(s_ref[row], jnp.concatenate([blocks_ref[p, q], blocks_ref[p, q + 1]], axis=1))
            return [(q, fold(moved[:, :nb]).astype(BF16)), (q + 1, fold(moved[:, nb:]).astype(BF16))]
        return [(q, fold(dot(s_ref[row], col_ref[p])).astype(BF16))]

    def stage(columns, q):
        def body(part, sums):
            sums = list(sums)
            for number, (j, dq) in enumerate(columns):
                source = cols_ref[j] + dq
                terms = []
                for k in range(group):
                    row = group * part + k
                    factor = splat_ref[(2 * j + dq) * 2 * fine_rows + row]
                    value = z_ref[row, source]
                    terms.append(value * jnp.concatenate([factor] * (value.shape[0] // 8), axis=0))
                sums[number] = sums[number] + tree(terms)
            if q is not None:
                results = []
                for k in range(group):
                    row = group * part + k
                    p = rows_ref[group // 2 * part + k // 2] + k % 2
                    results.append((row, spread(row, p, q)))
                for row, pieces in results:
                    for at, piece in pieces:
                        z_ref[row, at] = piece
            return tuple(sums)

        start = tuple(jnp.zeros(z_ref.shape[2:], BF16) for _ in columns)
        sums = lax.fori_loop(0, 2 * fine_rows // group, body, start)
        for number in range(0, len(columns), 2):
            j = columns[number][0]
            both = jnp.concatenate([unfold(part) for part in sums[number : number + 2]], axis=1)
            out_ref[:, j * nb : (j + 1) * nb] = dot(both, right_ref[j].reshape(2 * nb, nb)).astype(BF16)

    done = 0
    for number, q in enumerate(stages):
        ready = ends[number]
        for copy in waits[number]:
            copy.wait()
        stage([(j, dq) for j in range(done, ready) for dq in range(2)], q)
        done = ready


def share_kernel(parts_ref, image_ref, copies_ref):
    total = parts_ref[0].astype(F32)
    for k in range(1, parts_ref.shape[0]):
        total = total + parts_ref[k].astype(F32)
    image = total.astype(BF16)
    image_ref[...] = image
    for k in range(copies_ref.shape[0]):
        copies_ref[k] = image


def exchange(value, axis):
    return lax.all_to_all(value, axis, split_axis=0, concat_axis=0, tiled=True)


def call(kernel, name, spaces, outs, scratch, limit, flops, args):
    specs = {"s": SMEM, "v": VMEM, "h": pl.BlockSpec(memory_space=pltpu.HBM), "a": pl.BlockSpec(memory_space=pl.ANY)}
    size = sum(a.size * a.dtype.itemsize for a in args)
    return pl.pallas_call(
        kernel,
        out_shape=[jax.ShapeDtypeStruct(shape, kind) for shape, kind in outs],
        in_specs=[specs[space] for space in spaces],
        out_specs=[VMEM] * len(outs),
        scratch_shapes=scratch,
        cost_estimate=pl.CostEstimate(flops=flops, bytes_accessed=size, transcendentals=0),
        compiler_params=pltpu.CompilerParams(vmem_limit_bytes=limit * MIB),
        name=name,
    )(*args)


def body(
    coarse_kernel,
    left_rotation,
    right_rotation,
    fine_map,
    coefficient_index,
    coefficient_table,
    trial_vectors,
):
    n_rows = lax.axis_size("rowk")
    n_cols = lax.axis_size("colk")
    row_id = lax.axis_index("rowk")
    col_id = lax.axis_index("colk")
    coarse_total = coarse_kernel.shape[1]
    fine_rows = left_rotation.shape[0]
    fine_cols = right_rotation.shape[0]
    nb = left_rotation.shape[2]
    vecs = trial_vectors.shape[0]
    coarse_rows = coarse_total // n_rows
    coarse_cols = coarse_total // n_cols
    own = fine_rows // n_cols
    n_pairs = 2 * fine_cols
    dma = pltpu.SemaphoreType.DMA

    blocks = exchange(coarse_kernel.reshape(n_cols, coarse_cols, nb, nb), "colk")

    rows = lax.dynamic_slice_in_dim(fine_map, row_id * fine_rows, fine_rows) - row_id * coarse_rows
    cols = lax.dynamic_slice_in_dim(fine_map, col_id * fine_cols, fine_cols) - col_id * coarse_cols
    entries = jnp.arange(coefficient_table.shape[0], dtype=jnp.int32)
    table = jnp.where(entries > 0, coefficient_table, jnp.zeros_like(coefficient_table))
    edge = coefficient_index[:, fine_cols - 2 :, 1::2].transpose(0, 2, 1).reshape(-1)
    edge = jnp.sum(jnp.where(edge[:, None] == entries, table, jnp.zeros_like(table)), axis=-1)
    (u,) = call(rotate_kernel, "rotate", "vv", [((n_pairs, vecs, nb), F32)], [], 4, 10**8, (trial_vectors, right_rotation))
    foreign = shifted(edge, "colk", 1)
    foreign_u = shifted(jnp.stack([u[n_pairs - 3], u[n_pairs - 1]]), "colk", 1)
    source = (rows[:, None] + jnp.arange(2, dtype=jnp.int32)[None, :]).reshape(-1)
    numbers = jnp.arange(2 * fine_rows, dtype=jnp.int32)
    ahead = (source[None, :] < source[:, None]) | (
        (source[None, :] == source[:, None]) & (numbers[None, :] < numbers[:, None])
    )
    place = jnp.sum(ahead.astype(jnp.int32), axis=1)
    order = jnp.sum(jnp.where(place[None, :] == numbers[:, None], numbers[None, :], 0), axis=1)
    coarse = jnp.arange(coarse_rows + 1, dtype=jnp.int32)
    start = jnp.sum((source[None, :] < coarse[:, None]).astype(jnp.int32), axis=1)
    g, splat = call(
        prepare_kernel,
        "prepare",
        "ssssv",
        [((2 * fine_rows, vecs, coarse_cols * nb), BF16), ((2 * fine_rows * n_pairs, 8, 2 * nb), BF16)],
        [],
        24,
        10**9,
        (coefficient_index.reshape(-1), table, cols, order, u),
    )
    tied = lax.optimization_barrier((blocks, g, splat, rows, cols, place, order, start))
    blocks, g, splat, rows, cols, place, order, start = tied
    rim_row = shifted(blocks[0], "rowk", -1)
    rim_col = shifted(blocks[:, 0], "colk", -1)

    block_buffer = pltpu.VMEM((coarse_rows, coarse_cols, nb, nb), BF16)
    main, tail = call(
        forward_kernel,
        "forward",
        "ssssvhhh",
        [((n_cols, vecs, own * nb), BF16), ((own, vecs, coarse_cols * nb), BF16)],
        [
            pltpu.VMEM((2 * fine_rows + 8, vecs, coarse_cols * nb), BF16),
            block_buffer,
            pltpu.VMEM((2 * fine_rows + 8, vecs, nb), BF16),
            pltpu.VMEM(left_rotation.shape, BF16),
            dma((CHUNKS,)),
            dma((CHUNKS,)),
            dma((1,)),
        ],
        52,
        10**9,
        (order, place, start, foreign, foreign_u, left_rotation, g, blocks),
    )
    (partial,) = call(
        rim_kernel,
        "rim",
        "vvvva",
        [((n_cols, vecs, own * nb), BF16)],
        [],
        8,
        10**8,
        (main, tail, rim_row, left_rotation[fine_rows - own :, 1], rim_col),
    )
    corner = shifted(rim_row[0:1], "colk", -1)

    parts, corner = lax.optimization_barrier((exchange(partial, "colk"), corner))
    piece = (vecs, own * nb)
    forward_image, copies = call(
        share_kernel, "share", "v", [(piece, BF16), ((n_cols, *piece), BF16)], [], 8, 10**6, (parts,)
    )
    row_image = exchange(copies, "colk")

    (terms,) = call(
        adjoint_kernel,
        "adjoint",
        "ssvvvvvvhh",
        [((vecs, fine_cols * nb), BF16)],
        [
            pltpu.VMEM((2 * fine_rows, vecs, nb), BF16),
            pltpu.VMEM((2 * fine_rows, coarse_cols + 1, vecs // 2, 2 * nb), BF16),
            pltpu.VMEM((2 * fine_rows * n_pairs, 8, 2 * nb), BF16),
            pltpu.VMEM((coarse_rows + 1, coarse_cols, nb, nb), BF16),
            pltpu.VMEM((coarse_rows + 1, nb, nb), BF16),
            dma((coarse_cols + 4,)),
        ],
        52,
        10**9,
        (rows, cols, row_image, rim_row, rim_col, corner, left_rotation, right_rotation, splat, blocks),
    )

    terms = terms.reshape(n_rows, vecs // n_rows, fine_cols * nb)
    adjoint_image = jnp.sum(exchange(terms, "rowk").astype(F32), axis=0).astype(BF16)
    return (forward_image, adjoint_image)


def solution(mesh):
    return jax.shard_map(
        body,
        mesh=mesh,
        in_specs=(
            P(("rowk", "colk"), None, None, None),
            P("rowk", None, None, None),
            P("colk", None, None, None),
            P(),
            P("rowk", "colk", None),
            P(),
            P(None, "colk"),
        ),
        out_specs=(P(None, ("rowk", "colk")), P("rowk", "colk")),
        check_vma=False,
    )
```
